32 devices in a mesh: groups: 2 (over y), seq: 4 (over z), head: 2 (over x), cache: 2 (over core).
Axes of the slice: x: 2, y: 2, z: 4, core: 2. Of those that a mesh axis runs over, the one named last changes fastest.
Arguments:
- head_values: bfloat16 [2, 4096, 8192], P('groups', 'seq', ('head', 'cache')), parts along dimension 0, may hold values from -6 to 6
- gate_values: bfloat16 [2, 4096, 8192], P('groups', 'seq', ('head', 'cache')), parts along dimension 0, may hold values from -6 to 6
- state_inputs: bfloat16 [2, 4096, 8, 128], P('groups', 'seq', 'head'), parts along dimension 0, may hold values from -0.119628906 to 0.119628906
- state_readout: bfloat16 [2, 4096, 8, 128], P('groups', 'seq', 'head'), parts along dimension 0, may hold values from -6 to 6
- log_decays: float32 [2, 4096, 128], P('groups', 'seq', ('head', 'cache')), parts along dimension 0, may hold values from -1 to 0, as said below
- skip_gains: float32 [128], P(('head', 'cache')), may hold values from 0.5 to 2
- norm_gains: float32 [8192], P(('head', 'cache')), may hold values from 0.5 to 1.5
- cached_states: float32 [16, 128, 64, 128], P(('groups', 'seq'), ('head', 'cache')), parts along dimension 0, may hold values from -3 to 3
- owner_slots: int32 [16], P('groups'), parts along dimension 0, may hold values from 0 to 7, each once
- prefix_blocks: int32 [16], P('groups'), parts along dimension 0, may hold values from 1 to 3
- prompt_sessions: int32 [2], P('groups'), parts along dimension 0, may hold values from 0 to 7
Outputs:
- layer_output: bfloat16 [2, 4096, 8192], P('groups', 'seq', ('head', 'cache')), parts along dimension 0
The draws below stay inside these ranges and needn't reach their ends.
There are 2 independent parts, one for each index of `groups`. The reference program is written for one: setup_inputs(seed, part) draws one part's arguments, and reference() takes and returns one part's arrays. A program takes and returns all parts, laid end to end along the dimension named above; an argument that names none is the same for every part. Nothing has to cross between parts.
Inputs may be any that keep to these rules, and one draw needn't show every extreme that they name: owner_slots is a permutation of 0 to 7. `log_decays`: every entry is negative.
All inputs are finite; a program needn't handle non-finite values.
Results may differ from the reference program's by a relative error of at most 0.0042.
Values sent between devices are 32-bit elements; how exact they have to be, the bound alone decides.
A program may use at most 128 MiB of HBM per device.

```python
import jax
import jax.numpy as jnp
from jax import lax

HEAD_COUNT = 128
HEAD_DIM = 64
STATE = 128
GROUPS = 8
BLOCK = 1024
PROMPT_COUNT = 1
PROMPT_LENGTH = 4096
SESS = 8
N_SEQ = 4


def draw_log_decays(key, part):
    random_subkeys = jax.random.split(key, 7)
    slow_share = 0.5
    slow_draw = jax.random.uniform(random_subkeys[0], (HEAD_COUNT,))
    slow_rate = jnp.exp(jax.random.uniform(random_subkeys[1], (HEAD_COUNT,), jnp.float32, jnp.log(1e-06), jnp.log(3e-05)))
    fast_rate = jnp.exp(jax.random.uniform(random_subkeys[2], (HEAD_COUNT,), jnp.float32, jnp.log(0.003), jnp.log(0.04)))
    per_head_rate = jnp.where(slow_draw < slow_share, slow_rate, fast_rate)
    jaggedness = jnp.exp(jax.random.uniform(random_subkeys[3], (PROMPT_COUNT, PROMPT_LENGTH, HEAD_COUNT), jnp.float32, jnp.log(0.5), jnp.log(2.0)))
    block_wise = jnp.exp(jax.random.uniform(random_subkeys[4], (PROMPT_COUNT, PROMPT_LENGTH // BLOCK, 1), jnp.float32, jnp.log(0.5), jnp.log(2.0)))
    block_wise = jnp.repeat(block_wise, BLOCK, axis=1)
    spike_mask = jax.random.uniform(random_subkeys[5], (PROMPT_COUNT, PROMPT_LENGTH, HEAD_COUNT)) < 3.0 / PROMPT_LENGTH
    spike_penalty = jax.random.uniform(random_subkeys[6], (PROMPT_COUNT, PROMPT_LENGTH, HEAD_COUNT), jnp.float32, 0.2, 0.5)
    spike_events = jnp.where(spike_mask, jnp.log(1.0 - spike_penalty), 0.0)
    return (-(per_head_rate[None, None, :] * jaggedness * block_wise) + spike_events).astype(jnp.float32)


def place_ends(entries, stream_key, low, high):
    longest = entries.shape.index(max(entries.shape))
    spots = []
    for shift in (0, 1):
        where = [jax.random.randint(jax.random.fold_in(stream_key, axis), (), 0, length) for axis, length in enumerate(entries.shape)]
        where[longest] = (where[longest] + shift) % entries.shape[longest]
        spots.append(tuple(where))
    return entries.at[spots[0]].set(low).at[spots[1]].set(high)


def levels(rng, shape, pieces, smallest, top_value):
    gain = 1.0
    for position, parts in pieces:
        steps = jax.random.uniform(jax.random.fold_in(jax.random.fold_in(rng, 6), position), (parts,), jnp.float32, smallest / len(pieces), top_value / len(pieces))
        gain = gain * jnp.repeat(jnp.exp(steps), shape[position] // parts).reshape((-1,) + (1,) * (len(shape) - 1 - position))
    return gain


def scatter_about(own_key, shape, scale, bound, cuts=(), kind=jnp.bfloat16):
    drawn = jax.random.normal(own_key, shape, jnp.float32) * scale
    if len(cuts) > 0:
        drawn = levels(own_key, shape, cuts, -0.22, 0.18) * drawn
    return jnp.clip(drawn, min=-bound, max=bound).astype(kind)


def setup_inputs(seed: int = 0, part: int = 0) -> dict:
    seeds = jax.random.split(jax.random.key(seed), 12)
    own_keys = jax.random.split(jax.random.fold_in(seeds[11], part), 12)
    return {
        "head_values": scatter_about(own_keys[0], (PROMPT_COUNT, PROMPT_LENGTH, HEAD_COUNT * HEAD_DIM), 1.0, 6.0, ((1, 4), (2, 4))),
        "gate_values": scatter_about(own_keys[1], (PROMPT_COUNT, PROMPT_LENGTH, HEAD_COUNT * HEAD_DIM), 1.0, 6.0, ((1, 4), (2, 4))),
        "state_inputs": scatter_about(own_keys[2], (PROMPT_COUNT, PROMPT_LENGTH, GROUPS, STATE), 0.02, 0.119628906, ((1, 4), (2, 2))),
        "state_readout": scatter_about(own_keys[3], (PROMPT_COUNT, PROMPT_LENGTH, GROUPS, STATE), 1.0, 6.0, ((1, 4), (2, 2))),
        "log_decays": draw_log_decays(jax.random.fold_in(jax.random.fold_in(seeds[11], part), 71), part),
        "skip_gains": jnp.clip(0.5 + 1.5 * jax.random.uniform(seeds[5], (HEAD_COUNT,), jnp.float32) ** levels(seeds[5], (HEAD_COUNT,), ((0, 4),), -0.2, 0.2), 0.5, 2.0),
        "norm_gains": jnp.clip(1.0 + 0.1 * jax.random.normal(seeds[6], (HEAD_COUNT * HEAD_DIM,), jnp.float32), 0.5, 1.5),
        "cached_states": scatter_about(own_keys[7], (SESS, HEAD_COUNT, HEAD_DIM, STATE), 0.5, 3.0, ((0, 4), (1, 4)), jnp.float32),
        "owner_slots": jax.random.permutation(own_keys[8], SESS).astype(jnp.int32),
        "prefix_blocks": place_ends(jax.random.randint(own_keys[9], (SESS,), 1, N_SEQ), jax.random.fold_in(own_keys[9], 1), 1, N_SEQ - 1).astype(jnp.int32),
        "prompt_sessions": jax.random.randint(own_keys[10], (PROMPT_COUNT,), 0, SESS).astype(jnp.int32),
    }


def group_block(operands):
    value_rows, input_rows, readout_rows, decay_rows, state_carry = operands
    cumulative = jnp.cumsum(decay_rows, axis=0)
    scores = jnp.dot(readout_rows, input_rows.T, preferred_element_type=jnp.float32)
    positions = jnp.arange(BLOCK, dtype=jnp.int32)
    causal = positions[:, None] >= positions[None, :]
    spread = jnp.exp(jnp.where(causal[:, :, None], cumulative[:, None, :] - cumulative[None, :, :], -jnp.inf))
    mixing = (scores[:, :, None] * spread).astype(jnp.bfloat16)
    intra_term = jnp.einsum('tsh,shp->thp', mixing.astype(jnp.float32), value_rows.astype(jnp.float32))
    carried = jnp.einsum('tn,hpn->thp', readout_rows.astype(jnp.float32), state_carry, precision=lax.Precision.HIGHEST)
    carried = carried * jnp.exp(cumulative)[:, :, None]
    tail_decay = jnp.exp(cumulative[-1][None, :] - cumulative)
    scaled = (value_rows.astype(jnp.float32) * tail_decay[:, :, None]).astype(jnp.bfloat16)
    local_state = jnp.einsum('shp,sn->hpn', scaled.astype(jnp.float32), input_rows.astype(jnp.float32))
    return (intra_term + carried, local_state, jnp.exp(cumulative[-1]))

def reference(head_values, gate_values, state_inputs, state_readout, log_decays, skip_gains, norm_gains, cached_states, owner_slots, prefix_blocks, prompt_sessions):
    per_group = HEAD_COUNT // GROUPS
    block_count = PROMPT_LENGTH // BLOCK
    results = []
    for which_prompt in range(PROMPT_COUNT):
        session = prompt_sessions[which_prompt]
        cached_len = prefix_blocks[session]
        slot_row = owner_slots[session]
        cached = lax.dynamic_index_in_dim(cached_states, slot_row, 0, keepdims=False)
        cached = cached.reshape(GROUPS, per_group, HEAD_DIM, STATE)
        values = head_values[which_prompt].reshape(block_count, BLOCK, GROUPS, per_group, HEAD_DIM)
        gate_rows = gate_values[which_prompt].reshape(block_count, BLOCK, GROUPS, per_group, HEAD_DIM)
        inputs = state_inputs[which_prompt].reshape(block_count, BLOCK, GROUPS, STATE)
        readout = state_readout[which_prompt].reshape(block_count, BLOCK, GROUPS, STATE)
        decays = log_decays[which_prompt].reshape(block_count, BLOCK, GROUPS, per_group)

        def advance(state_carry, operands):
            block_index, value_rows, gate_block, input_rows, readout_rows, decay_rows = operands
            value_first = jnp.moveaxis(value_rows, 1, 0)
            gate_first = jnp.moveaxis(gate_block, 1, 0)
            ssd_term, local_states, endings = lax.map(group_block, (value_first, jnp.moveaxis(input_rows, 1, 0), jnp.moveaxis(readout_rows, 1, 0), jnp.moveaxis(decay_rows, 1, 0), state_carry))
            next_carry = endings[:, :, None, None] * state_carry + local_states
            next_carry = jnp.where(block_index == cached_len - 1, cached, next_carry)
            skip_term = skip_gains.reshape(GROUPS, 1, per_group, 1) * value_first.astype(jnp.float32)
            summed = jnp.where(block_index >= cached_len, ssd_term + skip_term, 0.0)
            gated = summed * jax.nn.silu(gate_first.astype(jnp.float32))
            mean_square = lax.optimization_barrier(jnp.mean(gated * gated, axis=3, keepdims=True))
            normed = gated * lax.rsqrt(mean_square + 1e-05) * norm_gains.reshape(GROUPS, 1, per_group, HEAD_DIM)
            return (next_carry, jnp.moveaxis(normed, 0, 1).reshape(BLOCK, HEAD_COUNT * HEAD_DIM).astype(jnp.bfloat16))
        initial = jnp.zeros((GROUPS, per_group, HEAD_DIM, STATE), jnp.float32)
        _, blocks_out = lax.scan(advance, initial, (jnp.arange(block_count, dtype=jnp.int32), values, gate_rows, inputs, readout, decays))
        results.append(blocks_out.reshape(PROMPT_LENGTH, HEAD_COUNT * HEAD_DIM))
    return jnp.stack(results)
```

```python
import functools

import jax
import jax.numpy as jnp
from jax import lax
from jax.experimental import pallas as pl
from jax.experimental.pallas import tpu as pltpu
from jax.sharding import PartitionSpec as P

HEAD_COUNT = 128
HEAD_DIM = 64
STATE = 128
GROUPS = 8
SUB = 128
PAIR = 2 * HEAD_DIM
LOG2E = 1.4426950408889634
F32 = jnp.float32
BF16 = jnp.bfloat16
MESH = pl.DeviceIdType.MESH


def split_rows(x):
    high = x.astype(BF16)
    low = (x - high.astype(F32)).astype(BF16)
    return jnp.concatenate([high, low], axis=0)


def kernel(
    n_seq, pairs, pairs_per_group, subs, owned_rows,
    sessions_ref, slots_ref, prefix_ref, skip_ref,
    inputs_ref, readout_ref, decays_ref, norm_ref, cached_ref, values_hbm, gates_hbm,
    out_hbm,
    vbuf, gbuf, obuf, acc, dec, own, bsend, brecv, fsend, frecv, local, ending,
    cum3, cum_t, cum_pad, scores, inputs_t, readout2,
    vsem, gsem, osem, bsend_sem, brecv_sem, fsend_sem, frecv_sem,
):
    me = lax.axis_index("seq")
    heads = 2 * pairs
    groups = pairs // pairs_per_group
    last = n_seq - 1

    def value_copy(c):
        return pltpu.make_async_copy(
            values_hbm.at[0, :, pl.ds(pl.multiple_of(c * PAIR, PAIR), PAIR)], vbuf.at[c], vsem.at[c]
        )

    def gate_copy(c):
        return pltpu.make_async_copy(
            gates_hbm.at[0, :, pl.ds(pl.multiple_of(c * PAIR, PAIR), PAIR)], gbuf.at[c], gsem.at[c]
        )

    def out_copy(c):
        return pltpu.make_async_copy(
            obuf.at[c], out_hbm.at[0, :, pl.ds(pl.multiple_of(c * PAIR, PAIR), PAIR)], osem.at[c]
        )

    def back_copy(src, c):
        return pltpu.make_async_remote_copy(
            src_ref=src.at[c], dst_ref=brecv.at[c], send_sem=bsend_sem.at[c],
            recv_sem=brecv_sem.at[c], device_id={"seq": me - 1}, device_id_type=MESH,
        )

    def forward_copy(src, c):
        return pltpu.make_async_remote_copy(
            src_ref=src.at[c], dst_ref=frecv.at[c], send_sem=fsend_sem.at[c],
            recv_sem=frecv_sem.at[c], device_id={"seq": me + 1}, device_id_type=MESH,
        )

    barrier = pltpu.get_barrier_semaphore()

    @pl.when(me > 0)
    def _():
        pl.semaphore_signal(barrier, inc=1, device_id={"seq": me - 1}, device_id_type=MESH)

    @pl.when(me < last)
    def _():
        pl.semaphore_signal(barrier, inc=1, device_id={"seq": me + 1}, device_id_type=MESH)

    @pl.loop(0, pairs)
    def _(c):
        value_copy(c).start()
        gate_copy(c).start()

    session = sessions_ref[0]
    slot = slots_ref[session]
    k = prefix_ref[session]
    owner = slot // owned_rows
    row_here = slot % owned_rows

    @pl.when((me > 0) & (me < last))
    def _():
        pl.semaphore_wait(barrier, 2)

    @pl.when((me == 0) | (me == last))
    def _():
        pl.semaphore_wait(barrier, 1)

    @pl.loop(0, pairs)
    def _(c):
        row = cached_ref[0, c]
        for other in range(1, owned_rows):
            row = jnp.where(row_here == other, cached_ref[other, c], row)
        row = row.T
        own[c] = row

        @pl.when(me == last)
        def _():
            bsend[c] = row
            back_copy(own, c).start()

        @pl.when(me == 0)
        def _():
            bsend[c] = row
            frecv[c] = row
            forward_copy(own, c).start()

    rows = lax.broadcasted_iota(jnp.int32, (SUB, SUB), 0)
    lanes = lax.broadcasted_iota(jnp.int32, (SUB, SUB), 1)
    causal = rows >= lanes
    tri = jnp.where(causal, 1.0, 0.0).astype(F32)
    for q in range(subs):
        at = pl.ds(q * SUB, SUB)
        cum = jnp.dot(
            tri, decays_ref[at, :] * LOG2E, precision=lax.Precision.HIGHEST,
            preferred_element_type=F32,
        )
        cum_pad[...] = jnp.zeros_like(cum_pad)
        cum_pad[:, :heads] = cum
        cum = cum_pad[...]
        cum_t[q] = cum.T
        high = cum.astype(BF16).astype(F32)
        middle = (cum - high).astype(BF16).astype(F32)
        low = (cum - high - middle).astype(BF16).astype(F32)
        cum3[at, :] = (
            high + pltpu.roll(middle, heads, axis=1) + pltpu.roll(low, 2 * heads, axis=1)
        ).astype(BF16)
        for g in range(groups):
            c_rows = readout_ref[g, at, :]
            b_rows = inputs_ref[g, at, :]
            product = lax.dot_general(
                c_rows, b_rows, (((1,), (1,)), ((), ())), preferred_element_type=F32
            )
            scores[g, q] = jnp.where(causal, product, 0.0)
            inputs_t[g, q] = b_rows.astype(F32).T.astype(BF16)
            readout2[g, at, :] = jnp.concatenate([c_rows, c_rows], axis=1)

    first_half = lanes < HEAD_DIM
    first_row = first_half[:1]
    spread_rows = lax.broadcasted_iota(jnp.int32, (128, 2 * SUB), 0)
    spread_lanes = lax.broadcasted_iota(jnp.int32, (128, 2 * SUB), 1)
    mean_of = jnp.where((rows < HEAD_DIM) == first_half, 1.0 / HEAD_DIM, 0.0).astype(BF16)

    def stage_one(c):
        g = c // pairs_per_group
        value_copy(c).wait()
        wanted = 2 * c + (spread_lanes >= SUB).astype(jnp.int32)
        pick = jnp.where(
            (spread_rows < 3 * heads) & ((spread_rows % heads) == wanted), 1.0, 0.0
        ).astype(BF16)
        skip_row = jnp.where(first_row, skip_ref[2 * c], skip_ref[2 * c + 1])
        state = None
        offset = jnp.zeros((1, PAIR), F32)
        for q in range(subs):
            at = pl.ds(q * SUB, SUB)
            cum = jnp.dot(cum3[at, :], pick, preferred_element_type=F32)
            cum0, cum1 = cum[:, :SUB], cum[:, SUB:]
            score = scores[g, q]
            mix0 = score * jnp.exp2(jnp.minimum(cum0 - cum_t[q, pl.ds(2 * c, 1), :], 0.0))
            mix1 = score * jnp.exp2(jnp.minimum(cum1 - cum_t[q, pl.ds(2 * c + 1, 1), :], 0.0))
            mix = jnp.concatenate([mix0.astype(BF16), mix1.astype(BF16)], axis=1)
            value = vbuf[c, at, :]
            value32 = value.astype(F32)
            zero = jnp.zeros_like(value32)
            both = jnp.concatenate(
                [
                    jnp.where(first_half, value32, zero).astype(BF16),
                    jnp.where(first_half, zero, value32).astype(BF16),
                ],
                axis=0,
            )
            total = jnp.dot(mix, both, preferred_element_type=F32) + skip_row * value32
            cum_p = jnp.where(first_half, cum0, cum1)
            end = cum_p[SUB - 1 :, :]
            decay = jnp.exp2(cum_p)
            if state is not None:
                total += decay * jnp.dot(
                    readout2[g, at, :], split_rows(state), preferred_element_type=F32
                )
            acc[c, at, :] = total
            dec[c, at, :] = decay * jnp.exp2(offset)
            scaled = (value32 * jnp.exp2(end - cum_p)).astype(BF16)
            here = jnp.dot(inputs_t[g, q], scaled, preferred_element_type=F32)
            state = here if state is None else jnp.exp2(end) * state + here
            offset = offset + end
        local[c] = state
        ending[c] = jnp.broadcast_to(jnp.exp2(offset), (8, PAIR))

    def back_step(c):
        back_copy(own, c).wait_recv()
        bsend[c] = jnp.where(owner == me, own[c], brecv[c])

        @pl.when(me >= 2)
        def _():
            back_copy(bsend, c).start()

    def finish(c):
        g = c // pairs_per_group

        @pl.when(me > 0)
        def _():
            forward_copy(own, c).wait_recv()

        below = frecv[c]
        cached = jnp.where(owner == me, own[c], jnp.where(owner > me, bsend[c], below))
        carry = jnp.where(me == k, cached, below)

        @pl.when((me > 0) & (me < last))
        def _():
            onward = ending[c, :1, :] * carry + local[c]
            fsend[c] = jnp.where(me < k, cached, onward)
            forward_copy(fsend, c).start()

        gate_copy(c).wait()
        carry2 = split_rows(carry)
        norm_row = norm_ref[pl.ds(c, 1), :]
        live = me >= k
        for q in range(subs):
            at = pl.ds(q * SUB, SUB)
            carried = jnp.dot(readout2[g, at, :], carry2, preferred_element_type=F32)
            summed = acc[c, at, :] + dec[c, at, :] * carried
            summed = jnp.where(live, summed, 0.0)
            gate = gbuf[c, at, :].astype(F32)
            half = 0.5 * gate
            gated = summed * (half + half * jnp.tanh(half))
            mean = jnp.dot((gated * gated).astype(BF16), mean_of, preferred_element_type=F32)
            obuf[c, at, :] = (gated * lax.rsqrt(mean + 1e-5) * norm_row).astype(BF16)
        out_copy(c).start()

    relays = (me > 0) & (me < last)
    ahead = jnp.where((me >= 2) & (me < last), jnp.minimum(pairs, 5 * (me - 1)), 0)

    @pl.loop(0, pairs + ahead)
    def _(step):
        @pl.when(step < pairs)
        def _():
            @pl.when(relays & (me >= 2))
            def _():
                back_step(step)

            stage_one(step)

            @pl.when(relays & (me < 2))
            def _():
                back_step(step)

        @pl.when(step >= ahead)
        def _():
            finish(step - ahead)

    @pl.loop(0, pairs)
    def _(c):
        out_copy(c).wait()

        @pl.when(me >= 2)
        def _():
            back_copy(own, c).wait_send()

        @pl.when(me < last)
        def _():
            forward_copy(own, c).wait_send()


def on_device(
    n_seq,
    head_values,
    gate_values,
    state_inputs,
    state_readout,
    log_decays,
    skip_gains,
    norm_gains,
    cached_states,
    owner_slots,
    prefix_blocks,
    prompt_sessions,
):
    _, block, width = head_values.shape
    heads = width // HEAD_DIM
    per_group = HEAD_COUNT // GROUPS
    groups = max(1, heads // per_group)
    pairs = heads // 2
    subs = block // SUB
    owned = cached_states.shape[0]
    first = lax.axis_index("cache") * heads // per_group
    inputs = jnp.moveaxis(lax.dynamic_slice_in_dim(state_inputs, first, groups, 2)[0], 1, 0)
    readout = jnp.moveaxis(lax.dynamic_slice_in_dim(state_readout, first, groups, 2)[0], 1, 0)
    smem = pl.BlockSpec(memory_space=pltpu.SMEM)
    vmem = pl.BlockSpec(memory_space=pltpu.VMEM)
    hbm = pl.BlockSpec(memory_space=pl.ANY)
    tiles = pltpu.VMEM((pairs, STATE, PAIR), F32)
    sems = pltpu.SemaphoreType.DMA((pairs,))
    return pl.pallas_call(
        functools.partial(kernel, n_seq, pairs, pairs // groups, subs, owned),
        out_shape=jax.ShapeDtypeStruct(head_values.shape, BF16),
        in_specs=[smem] * 4 + [vmem] * 5 + [hbm] * 2,
        out_specs=hbm,
        scratch_shapes=[
            pltpu.VMEM((pairs, block, PAIR), BF16),
            pltpu.VMEM((pairs, block, PAIR), BF16),
            pltpu.VMEM((pairs, block, PAIR), BF16),
            pltpu.VMEM((pairs, block, PAIR), F32),
            pltpu.VMEM((pairs, block, PAIR), F32),
            tiles, tiles, tiles, tiles, tiles, tiles,
            pltpu.VMEM((pairs, 8, PAIR), F32),
            pltpu.VMEM((block, 128), BF16),
            pltpu.VMEM((subs, 128, SUB), F32),
            pltpu.VMEM((SUB, 128), F32),
            pltpu.VMEM((groups, subs, SUB, SUB), F32),
            pltpu.VMEM((groups, subs, STATE, SUB), BF16),
            pltpu.VMEM((groups, block, 2 * STATE), BF16),
            sems, sems, sems, sems, sems, sems, sems,
        ],
        compiler_params=pltpu.CompilerParams(
            collective_id=0, has_side_effects=True, vmem_limit_bytes=58 * 1024 * 1024
        ),
        name="scan_chain",
    )(
        prompt_sessions, owner_slots, prefix_blocks, skip_gains,
        inputs, readout, log_decays[0], norm_gains.reshape(pairs, PAIR),
        cached_states.reshape(owned, pairs, PAIR, STATE), head_values, gate_values,
    )


def solution(mesh):
    in_specs = (
        P("groups", "seq", ("head", "cache")),
        P("groups", "seq", ("head", "cache")),
        P("groups", "seq", "head", None),
        P("groups", "seq", "head", None),
        P("groups", "seq", ("head", "cache")),
        P(("head", "cache")),
        P(("head", "cache")),
        P(("groups", "seq"), ("head", "cache"), None, None),
        P("groups"),
        P("groups"),
        P("groups"),
    )
    return jax.shard_map(
        functools.partial(on_device, mesh.shape["seq"]), mesh=mesh, in_specs=in_specs,
        out_specs=P("groups", "seq", ("head", "cache")), check_vma=False,
    )
```

```python
import functools

import jax
import jax.numpy as jnp
from jax import lax
from jax.experimental import pallas as pl
from jax.experimental.pallas import tpu as pltpu
from jax.sharding import PartitionSpec as P

HEAD_COUNT = 128
HEAD_DIM = 64
STATE = 128
GROUPS = 8
SUB = 128
PAIR = 2 * HEAD_DIM
LOG2E = 1.4426950408889634
QUAD = 2 * PAIR
F32 = jnp.float32
BF16 = jnp.bfloat16
MESH = pl.DeviceIdType.MESH


def split_rows(x):
    high = x.astype(BF16)
    low = (x - high.astype(F32)).astype(BF16)
    return jnp.concatenate([high, low], axis=0)


def kernel(
    n_seq, pairs, pairs_per_group, subs, owned_rows,
    sessions_ref, slots_ref, prefix_ref, skip_ref,
    *refs,
):
    me = lax.axis_index("seq")
    heads = 2 * pairs
    groups = pairs // pairs_per_group
    inputs_refs, readout_refs = refs[:groups], refs[groups : 2 * groups]
    (
        decays_ref, norm_ref, cached_ref, values_hbm, gates_hbm, out_hbm, live_ref,
        vbuf, gbuf, obuf, acc, dec, own, bsend, brecv, fsend, frecv, local, ending,
        cum3, cum_t, cum_pad, scores, inputs_t, readout2, spread, big, squares,
        vsem, gsem, osem, bsend_sem, brecv_sem, fsend_sem, frecv_sem,
    ) = refs[2 * groups :]
    last = n_seq - 1

    def value_copy(c):
        return pltpu.make_async_copy(
            values_hbm.at[0, :, pl.ds(pl.multiple_of(c * PAIR, PAIR), PAIR)], vbuf.at[c], vsem.at[c]
        )

    def gate_copy(c):
        return pltpu.make_async_copy(
            gates_hbm.at[0, :, pl.ds(pl.multiple_of(c * PAIR, PAIR), PAIR)], gbuf.at[c], gsem.at[c]
        )

    def out_copy(c):
        return pltpu.make_async_copy(
            obuf.at[c], out_hbm.at[0, :, pl.ds(pl.multiple_of(c * PAIR, PAIR), PAIR)], osem.at[c]
        )

    def back_copy(src, c):
        return pltpu.make_async_remote_copy(
            src_ref=src.at[c], dst_ref=brecv.at[c], send_sem=bsend_sem.at[c],
            recv_sem=brecv_sem.at[c], device_id={"seq": me - 1}, device_id_type=MESH,
        )

    def forward_copy(src, c):
        return pltpu.make_async_remote_copy(
            src_ref=src.at[c], dst_ref=frecv.at[c], send_sem=fsend_sem.at[c],
            recv_sem=frecv_sem.at[c], device_id={"seq": me + 1}, device_id_type=MESH,
        )

    barrier = pltpu.get_barrier_semaphore()

    @pl.when(me > 0)
    def _():
        pl.semaphore_signal(barrier, inc=1, device_id={"seq": me - 1}, device_id_type=MESH)

    @pl.when(me < last)
    def _():
        pl.semaphore_signal(barrier, inc=1, device_id={"seq": me + 1}, device_id_type=MESH)

    @pl.loop(0, pairs)
    def _(c):
        value_copy(c).start()
        gate_copy(c).start()

    session = sessions_ref[0]
    slot = slots_ref[session]
    k = prefix_ref[session]
    owner = slot // owned_rows
    row_here = slot % owned_rows
    live_ref[0] = (me >= k).astype(jnp.int32)

    @pl.when((me > 0) & (me < last))
    def _():
        pl.semaphore_wait(barrier, 2)

    @pl.when((me == 0) | (me == last))
    def _():
        pl.semaphore_wait(barrier, 1)

    @pl.loop(0, pairs)
    def _(c):
        row = cached_ref[0, c]
        for other in range(1, owned_rows):
            row = jnp.where(row_here == other, cached_ref[other, c], row)
        row = row.T
        own[c] = row

        @pl.when(me == last)
        def _():
            bsend[c] = row
            back_copy(own, c).start()

        @pl.when(me == 0)
        def _():
            bsend[c] = row
            frecv[c] = row
            forward_copy(own, c).start()

    rows = lax.broadcasted_iota(jnp.int32, (SUB, SUB), 0)
    lanes = lax.broadcasted_iota(jnp.int32, (SUB, SUB), 1)
    causal = rows >= lanes
    tri = jnp.where(rows <= lanes, 1.0, 0.0).astype(F32)
    cum_pad[...] = jnp.zeros_like(cum_pad)
    for q in range(subs):
        at = pl.ds(q * SUB, SUB)
        sums = jnp.dot(
            decays_ref[:, at] * LOG2E, tri, precision=lax.Precision.HIGHEST,
            preferred_element_type=F32,
        )
        cum_t[q] = sums
        cum_pad[:heads, :] = sums
        cum = cum_pad[...].T
        high = cum.astype(BF16).astype(F32)
        middle = (cum - high).astype(BF16).astype(F32)
        low = (cum - high - middle).astype(BF16).astype(F32)
        cum3[at, :] = (
            high + pltpu.roll(middle, heads, axis=1) + pltpu.roll(low, 2 * heads, axis=1)
        ).astype(BF16)
        for g in range(groups):
            c_rows = readout_refs[g][at, :]
            b_rows = inputs_refs[g][at, :]
            product = lax.dot_general(
                c_rows, b_rows, (((1,), (1,)), ((), ())), preferred_element_type=F32
            )
            scores[g, q] = jnp.where(causal, product, 0.0)
            inputs_t[g, q] = b_rows.astype(F32).T.astype(BF16)
            readout2[g, at, :] = jnp.concatenate([c_rows, c_rows], axis=1)

    wide_rows = lax.broadcasted_iota(jnp.int32, (QUAD, QUAD), 0)
    wide_lanes = lax.broadcasted_iota(jnp.int32, (QUAD, QUAD), 1)
    first_half = lanes < HEAD_DIM
    wide_half = (wide_lanes[:SUB] % PAIR) < HEAD_DIM
    row_half = wide_half[:1]
    spread_rows = lax.broadcasted_iota(jnp.int32, (128, 4 * SUB), 0)
    spread_lanes = lax.broadcasted_iota(jnp.int32, (128, 4 * SUB), 1)
    mean_of = jnp.where(
        wide_rows // HEAD_DIM == wide_lanes // HEAD_DIM, 1.0 / HEAD_DIM, 0.0
    ).astype(BF16)

    def stage_one(u):
        g = (2 * u) // pairs_per_group
        value_copy(2 * u).wait()
        value_copy(2 * u + 1).wait()
        wanted = 4 * u + spread_lanes // SUB
        pick = jnp.where(
            (spread_rows < 3 * heads) & ((spread_rows % heads) == wanted), 1.0, 0.0
        ).astype(BF16)
        spread[...] = jnp.dot(cum3[...], pick, preferred_element_type=F32)
        low_pair = jnp.where(row_half, skip_ref[4 * u], skip_ref[4 * u + 1])
        high_pair = jnp.where(row_half, skip_ref[4 * u + 2], skip_ref[4 * u + 3])
        skip_row = jnp.where(wide_lanes[:1] < PAIR, low_pair, high_pair)
        state = None
        offset = jnp.zeros((1, QUAD), F32)
        for q in range(subs):
            at = pl.ds(q * SUB, SUB)
            score = scores[g, q]
            intra, values, cums = [], [], []
            for p in range(2):
                cum0 = spread[at, 2 * p * SUB : (2 * p + 1) * SUB]
                cum1 = spread[at, (2 * p + 1) * SUB : (2 * p + 2) * SUB]
                row0 = cum_t[q, pl.ds(4 * u + 2 * p, 1), :]
                row1 = cum_t[q, pl.ds(4 * u + 2 * p + 1, 1), :]
                mix0 = score * jnp.exp2(jnp.minimum(cum0 - row0, 0.0))
                mix1 = score * jnp.exp2(jnp.minimum(cum1 - row1, 0.0))
                mix = jnp.concatenate([mix0.astype(BF16), mix1.astype(BF16)], axis=1)
                value32 = vbuf[2 * u + p, at, :].astype(F32)
                both = jnp.concatenate(
                    [
                        jnp.where(first_half, value32, 0.0).astype(BF16),
                        jnp.where(first_half, 0.0, value32).astype(BF16),
                    ],
                    axis=0,
                )
                intra.append(jnp.dot(mix, both, preferred_element_type=F32))
                values.append(value32)
                cums.append(jnp.where(first_half, cum0, cum1))
            value = jnp.concatenate(values, axis=1)
            cum_p = jnp.concatenate(cums, axis=1)
            total = jnp.concatenate(intra, axis=1) + skip_row * value
            end = cum_p[SUB - 1 :, :]
            decay = jnp.exp2(cum_p)
            if state is not None:
                total += decay * jnp.dot(
                    readout2[g, at, :], split_rows(state), preferred_element_type=F32
                )
            acc[u, at, :] = total
            dec[u, at, :] = decay * jnp.exp2(offset)
            scaled = (value * jnp.exp2(end - cum_p)).astype(BF16)
            here = jnp.dot(inputs_t[g, q], scaled, preferred_element_type=F32)
            state = here if state is None else jnp.exp2(end) * state + here
            offset = offset + end
        local[2 * u] = state[:, :PAIR]
        local[2 * u + 1] = state[:, PAIR:]
        final = jnp.exp2(offset)
        ending[2 * u] = jnp.broadcast_to(final[:, :PAIR], (8, PAIR))
        ending[2 * u + 1] = jnp.broadcast_to(final[:, PAIR:], (8, PAIR))

    def back_step(c):
        back_copy(own, c).wait_recv()
        bsend[c] = jnp.where(owner == me, own[c], brecv[c])

        @pl.when(me >= 2)
        def _():
            back_copy(bsend, c).start()

    relays = (me > 0) & (me < last)

    def carry_step(c):
        @pl.when(me == 1)
        def _():
            back_step(c)

        @pl.when(me > 0)
        def _():
            forward_copy(own, c).wait_recv()

        below = frecv[c]
        cached = jnp.where(owner == me, own[c], jnp.where(owner > me, bsend[c], below))
        carry = jnp.where(me == k, cached, below)

        @pl.when(relays)
        def _():
            onward = ending[c, :1, :] * carry + local[c]
            fsend[c] = jnp.where(me < k, cached, onward)
            forward_copy(fsend, c).start()

        local[c] = carry

    def finish(u):
        g = (2 * u) // pairs_per_group
        gate_copy(2 * u).wait()
        gate_copy(2 * u + 1).wait()
        carry = jnp.concatenate([local[2 * u], local[2 * u + 1]], axis=1)
        big[...] = jnp.dot(readout2[g], split_rows(carry), preferred_element_type=F32)
        for q in range(subs):
            at = pl.ds(q * SUB, SUB)
            summed = acc[u, at, :] + dec[u, at, :] * big[at, :]
            gate = jnp.concatenate([gbuf[2 * u, at, :], gbuf[2 * u + 1, at, :]], axis=1)
            half = 0.5 * gate.astype(F32)
            gated = summed * (half + half * jnp.tanh(half))
            squares[at, :] = (gated * gated).astype(BF16)
            acc[u, at, :] = gated
        big[...] = jnp.dot(squares[...], mean_of, preferred_element_type=F32)
        norm_row = jnp.concatenate(
            [norm_ref[pl.ds(2 * u, 1), :], norm_ref[pl.ds(2 * u + 1, 1), :]], axis=1
        )
        for q in range(subs):
            at = pl.ds(q * SUB, SUB)
            normed = (acc[u, at, :] * lax.rsqrt(big[at, :] + 1e-5) * norm_row).astype(BF16)
            obuf[2 * u, at, :] = normed[:, :PAIR]
            obuf[2 * u + 1, at, :] = normed[:, PAIR:]
        out_copy(2 * u).start()
        out_copy(2 * u + 1).start()

    units = pairs // 2
    carry_lag = jnp.where(relays, jnp.minimum(units, 2 * me - 1), 0)
    carry_lag = jnp.where(me == last, jnp.minimum(units, 2 * me - 2), carry_lag)
    finish_lag = jnp.where(relays, carry_lag + 2, carry_lag)

    @pl.loop(0, units + finish_lag)
    def _(step):
        @pl.when(step < units)
        def _():
            @pl.when(relays & (me >= 2))
            def _():
                back_step(2 * step)
                back_step(2 * step + 1)

            stage_one(step)

        @pl.when((step >= carry_lag) & (step < units + carry_lag))
        def _():
            carry_step(2 * (step - carry_lag))
            carry_step(2 * (step - carry_lag) + 1)

        @pl.when(step >= finish_lag)
        def _():
            finish(step - finish_lag)

    @pl.loop(0, pairs)
    def _(c):
        out_copy(c).wait()

        @pl.when(me >= 2)
        def _():
            back_copy(own, c).wait_send()

        @pl.when(me < last)
        def _():
            forward_copy(own, c).wait_send()


def on_device(
    n_seq,
    n_cache,
    head_values,
    gate_values,
    state_inputs,
    state_readout,
    log_decays,
    skip_gains,
    norm_gains,
    cached_states,
    owner_slots,
    prefix_blocks,
    prompt_sessions,
):
    _, block, width = head_values.shape
    heads = width // HEAD_DIM
    per_group = HEAD_COUNT // GROUPS
    groups = max(1, heads // per_group)
    pairs = heads // 2
    subs = block // SUB
    owned = cached_states.shape[0]
    cache_index = lax.axis_index("cache")

    def group_rows(array, which):
        rows = array[0, :, which]
        for index in range(1, n_cache):
            rows = jnp.where(
                cache_index == index, array[0, :, index * heads // per_group + which], rows
            )
        return rows

    inputs = [group_rows(state_inputs, g) for g in range(groups)]
    readout = [group_rows(state_readout, g) for g in range(groups)]
    smem = pl.BlockSpec(memory_space=pltpu.SMEM)
    vmem = pl.BlockSpec(memory_space=pltpu.VMEM)
    hbm = pl.BlockSpec(memory_space=pl.ANY)
    tiles = pltpu.VMEM((pairs, STATE, PAIR), F32)
    sems = pltpu.SemaphoreType.DMA((pairs,))
    out, live = pl.pallas_call(
        functools.partial(kernel, n_seq, pairs, pairs // groups, subs, owned),
        out_shape=(
            jax.ShapeDtypeStruct(head_values.shape, BF16),
            jax.ShapeDtypeStruct((1,), jnp.int32),
        ),
        in_specs=[smem] * 4 + [vmem] * (3 + 2 * groups) + [hbm] * 2,
        out_specs=(hbm, smem),
        scratch_shapes=[
            pltpu.VMEM((pairs, block, PAIR), BF16),
            pltpu.VMEM((pairs, block, PAIR), BF16),
            pltpu.VMEM((pairs, block, PAIR), BF16),
            pltpu.VMEM((pairs // 2, block, QUAD), F32),
            pltpu.VMEM((pairs // 2, block, QUAD), F32),
            tiles, tiles, tiles, tiles, tiles, tiles,
            pltpu.VMEM((pairs, 8, PAIR), F32),
            pltpu.VMEM((block, 128), BF16),
            pltpu.VMEM((subs, heads, SUB), F32),
            pltpu.VMEM((128, SUB), F32),
            pltpu.VMEM((groups, subs, SUB, SUB), F32),
            pltpu.VMEM((groups, subs, STATE, SUB), BF16),
            pltpu.VMEM((groups, block, 2 * STATE), BF16),
            pltpu.VMEM((block, 4 * SUB), F32),
            pltpu.VMEM((block, QUAD), F32),
            pltpu.VMEM((block, QUAD), BF16),
            sems, sems, sems, sems, sems, sems, sems,
        ],
        compiler_params=pltpu.CompilerParams(
            collective_id=0, has_side_effects=True, vmem_limit_bytes=58 * 1024 * 1024
        ),
        name="scan_chain",
    )(
        prompt_sessions, owner_slots, prefix_blocks, skip_gains,
        *inputs, *readout, log_decays[0].T, norm_gains.reshape(pairs, PAIR),
        cached_states.reshape(owned, pairs, PAIR, STATE), head_values, gate_values,
    )
    return jnp.where(live[0] > 0, out, jnp.zeros_like(out))


def solution(mesh):
    in_specs = (
        P("groups", "seq", ("head", "cache")),
        P("groups", "seq", ("head", "cache")),
        P("groups", "seq", "head", None),
        P("groups", "seq", "head", None),
        P("groups", "seq", ("head", "cache")),
        P(("head", "cache")),
        P(("head", "cache")),
        P(("groups", "seq"), ("head", "cache"), None, None),
        P("groups"),
        P("groups"),
        P("groups"),
    )
    return jax.shard_map(
        functools.partial(on_device, mesh.shape["seq"], mesh.shape["cache"]), mesh=mesh, in_specs=in_specs,
        out_specs=P("groups", "seq", ("head", "cache")), check_vma=False,
    )
```

```python
import functools

import jax
import jax.numpy as jnp
from jax import lax
from jax.experimental import pallas as pl
from jax.experimental.pallas import tpu as pltpu
from jax.sharding import PartitionSpec as P

HEAD_COUNT = 128
HEAD_DIM = 64
STATE = 128
GROUPS = 8
SUB = 128
PAIR = 2 * HEAD_DIM
LOG2E = 1.4426950408889634
QUAD = 2 * PAIR
F32 = jnp.float32
BF16 = jnp.bfloat16
MESH = pl.DeviceIdType.MESH


def split_rows(x):
    high = x.astype(BF16)
    low = (x - high.astype(F32)).astype(BF16)
    return jnp.concatenate([high, low], axis=0)


def kernel(
    n_seq, pairs, pairs_per_group, per_group, subs, owned_rows,
    sessions_ref, slots_ref, prefix_ref, skip_ref,
    *refs,
):
    me = lax.axis_index("seq")
    heads = 2 * pairs
    groups = pairs // pairs_per_group
    first_group = lax.axis_index("cache") * heads // per_group
    (
        inputs_ref, readout_ref, decays_ref, norm_ref, cached_ref, values_hbm, gates_hbm, out_hbm, live_ref,
        vbuf, gbuf, obuf, acc, dec, own, bsend, brecv, fsend, frecv, local, ending,
        cum3, cum_t, cum_pad, scores, inputs_t, readout2, spread, big, squares, staged,
        vsem, gsem, osem, bsend_sem, brecv_sem, fsend_sem, frecv_sem,
    ) = refs
    last = n_seq - 1

    def value_copy(c):
        return pltpu.make_async_copy(
            values_hbm.at[0, :, pl.ds(pl.multiple_of(c * PAIR, PAIR), PAIR)], vbuf.at[c], vsem.at[c]
        )

    def gate_copy(c):
        return pltpu.make_async_copy(
            gates_hbm.at[0, :, pl.ds(pl.multiple_of(c * PAIR, PAIR), PAIR)], gbuf.at[c], gsem.at[c]
        )

    def out_copy(c):
        return pltpu.make_async_copy(
            obuf.at[c], out_hbm.at[0, :, pl.ds(pl.multiple_of(c * PAIR, PAIR), PAIR)], osem.at[c]
        )

    def back_copy(src, c):
        return pltpu.make_async_remote_copy(
            src_ref=src.at[c], dst_ref=brecv.at[c], send_sem=bsend_sem.at[c],
            recv_sem=brecv_sem.at[c], device_id={"seq": me - 1}, device_id_type=MESH,
        )

    def forward_copy(src, c):
        return pltpu.make_async_remote_copy(
            src_ref=src.at[c], dst_ref=frecv.at[c], send_sem=fsend_sem.at[c],
            recv_sem=frecv_sem.at[c], device_id={"seq": me + 1}, device_id_type=MESH,
        )

    barrier = pltpu.get_barrier_semaphore()

    @pl.when(me > 0)
    def _():
        pl.semaphore_signal(barrier, inc=1, device_id={"seq": me - 1}, device_id_type=MESH)

    @pl.when(me < last)
    def _():
        pl.semaphore_signal(barrier, inc=1, device_id={"seq": me + 1}, device_id_type=MESH)

    @pl.loop(0, pairs)
    def _(c):
        value_copy(c).start()
        gate_copy(c).start()

    session = sessions_ref[0]
    slot = slots_ref[session]
    k = prefix_ref[session]
    owner = slot // owned_rows
    row_here = slot % owned_rows
    live_ref[0] = (me >= k).astype(jnp.int32)

    @pl.when((me > 0) & (me < last))
    def _():
        pl.semaphore_wait(barrier, 2)

    @pl.when((me == 0) | (me == last))
    def _():
        pl.semaphore_wait(barrier, 1)

    @pl.loop(0, pairs)
    def _(c):
        row = cached_ref[0, c]
        for other in range(1, owned_rows):
            row = jnp.where(row_here == other, cached_ref[other, c], row)
        row = row.T
        own[c] = row

        @pl.when(me == last)
        def _():
            bsend[c] = row
            back_copy(own, c).start()

        @pl.when(me == 0)
        def _():
            bsend[c] = row
            frecv[c] = jnp.zeros((STATE + 8, PAIR), F32)
            fsend[c, :STATE, :] = row
            fsend[c, STATE:, :] = jnp.zeros((8, PAIR), F32)
            forward_copy(fsend, c).start()

    rows = lax.broadcasted_iota(jnp.int32, (SUB, SUB), 0)
    lanes = lax.broadcasted_iota(jnp.int32, (SUB, SUB), 1)
    causal = rows >= lanes
    tri = jnp.where(rows <= lanes, 1.0, 0.0).astype(F32)
    cum_pad[...] = jnp.zeros_like(cum_pad)
    for q in range(subs):
        at = pl.ds(q * SUB, SUB)
        sums = jnp.dot(
            decays_ref[:, at] * LOG2E, tri, precision=lax.Precision.HIGHEST,
            preferred_element_type=F32,
        )
        cum_t[q] = sums
        cum_pad[:heads, :] = sums
        cum = cum_pad[...].T
        high = cum.astype(BF16).astype(F32)
        middle = (cum - high).astype(BF16).astype(F32)
        low = (cum - high - middle).astype(BF16).astype(F32)
        cum3[at, :] = (
            high + pltpu.roll(middle, heads, axis=1) + pltpu.roll(low, 2 * heads, axis=1)
        ).astype(BF16)
        for which, raw in enumerate((inputs_ref, readout_ref)):
            staged[which] = raw[at].astype(F32).reshape(SUB * raw.shape[1], STATE)
        step = inputs_ref.shape[1]
        for g in range(groups):
            mine = pl.ds(first_group + g, SUB, stride=step)
            b_rows32 = staged[0, mine, :]
            b_rows = b_rows32.astype(BF16)
            c_rows = staged[1, mine, :].astype(BF16)
            product = lax.dot_general(
                c_rows, b_rows, (((1,), (1,)), ((), ())), preferred_element_type=F32
            )
            scores[g, q] = jnp.where(causal, product, 0.0)
            inputs_t[g, q] = b_rows32.T.astype(BF16)
            readout2[g, at, :] = jnp.concatenate([c_rows, c_rows], axis=1)

    wide_rows = lax.broadcasted_iota(jnp.int32, (QUAD, QUAD), 0)
    wide_lanes = lax.broadcasted_iota(jnp.int32, (QUAD, QUAD), 1)
    first_half = lanes < HEAD_DIM
    wide_half = (wide_lanes[:SUB] % PAIR) < HEAD_DIM
    row_half = wide_half[:1]
    spread_rows = lax.broadcasted_iota(jnp.int32, (128, 4 * SUB), 0)
    spread_lanes = lax.broadcasted_iota(jnp.int32, (128, 4 * SUB), 1)
    mean_of = jnp.where(
        wide_rows // HEAD_DIM == wide_lanes // HEAD_DIM, 1.0 / HEAD_DIM, 0.0
    ).astype(BF16)

    def stage_one(u):
        g = (2 * u) // pairs_per_group
        value_copy(2 * u).wait()
        value_copy(2 * u + 1).wait()
        wanted = 4 * u + spread_lanes // SUB
        pick = jnp.where(
            (spread_rows < 3 * heads) & ((spread_rows % heads) == wanted), 1.0, 0.0
        ).astype(BF16)
        spread[...] = jnp.dot(cum3[...], pick, preferred_element_type=F32)
        low_pair = jnp.where(row_half, skip_ref[4 * u], skip_ref[4 * u + 1])
        high_pair = jnp.where(row_half, skip_ref[4 * u + 2], skip_ref[4 * u + 3])
        skip_row = jnp.where(wide_lanes[:1] < PAIR, low_pair, high_pair)
        state = None
        offset = jnp.zeros((1, QUAD), F32)
        for q in range(subs):
            at = pl.ds(q * SUB, SUB)
            score = scores[g, q]
            intra, values, cums = [], [], []
            for p in range(2):
                cum0 = spread[at, 2 * p * SUB : (2 * p + 1) * SUB]
                cum1 = spread[at, (2 * p + 1) * SUB : (2 * p + 2) * SUB]
                row0 = cum_t[q, pl.ds(4 * u + 2 * p, 1), :]
                row1 = cum_t[q, pl.ds(4 * u + 2 * p + 1, 1), :]
                mix0 = score * jnp.exp2(jnp.minimum(cum0 - row0, 0.0))
                mix1 = score * jnp.exp2(jnp.minimum(cum1 - row1, 0.0))
                mix = jnp.concatenate([mix0.astype(BF16), mix1.astype(BF16)], axis=1)
                value32 = vbuf[2 * u + p, at, :].astype(F32)
                both = jnp.concatenate(
                    [
                        jnp.where(first_half, value32, 0.0).astype(BF16),
                        jnp.where(first_half, 0.0, value32).astype(BF16),
                    ],
                    axis=0,
                )
                intra.append(jnp.dot(mix, both, preferred_element_type=F32))
                values.append(value32)
                cums.append(jnp.where(first_half, cum0, cum1))
            value = jnp.concatenate(values, axis=1)
            cum_p = jnp.concatenate(cums, axis=1)
            total = jnp.concatenate(intra, axis=1) + skip_row * value
            end = cum_p[SUB - 1 :, :]
            decay = jnp.exp2(cum_p)
            if state is not None:
                total += decay * jnp.dot(
                    readout2[g, at, :], split_rows(state), preferred_element_type=F32
                )
            acc[u, at, :] = total
            dec[u, at, :] = decay * jnp.exp2(offset)
            scaled = (value * jnp.exp2(end - cum_p)).astype(BF16)
            here = jnp.dot(inputs_t[g, q], scaled, preferred_element_type=F32)
            state = here if state is None else jnp.exp2(end) * state + here
            offset = offset + end
        local[2 * u] = state[:, :PAIR]
        local[2 * u + 1] = state[:, PAIR:]
        final = jnp.exp2(offset)
        ending[2 * u] = jnp.broadcast_to(final[:, :PAIR], (8, PAIR))
        ending[2 * u + 1] = jnp.broadcast_to(final[:, PAIR:], (8, PAIR))

    def back_step(c):
        back_copy(own, c).wait_recv()
        bsend[c] = jnp.where(owner == me, own[c], brecv[c])

        @pl.when(me >= 2)
        def _():
            back_copy(bsend, c).start()

    relays = (me > 0) & (me < last)

    def carry_step(c):
        @pl.when(me > 0)
        def _():
            forward_copy(fsend, c).wait_recv()

        below = frecv[c, :STATE, :]
        factor = frecv[c, STATE:, :]

        @pl.when(relays)
        def _():
            cached = jnp.where(owner == me, own[c], below)
            added = jnp.where(owner == me, below + factor[:1] * own[c], below)
            start = jnp.where(me == k, jnp.where(owner <= me, cached, 0.0), added)
            onward = ending[c, :1, :] * start + local[c]
            fsend[c, :STATE, :] = jnp.where(me < k, cached, onward)
            fsend[c, STATE:, :] = ending[c] * jnp.where(me == k, 1.0, factor)
            forward_copy(fsend, c).start()

    def carry_of(c):
        @pl.when(me == 1)
        def _():
            back_step(c)

        below = frecv[c, :STATE, :]
        above = bsend[c]
        later = jnp.where(owner >= me, below + frecv[c, STATE : STATE + 1, :] * above, below)
        return jnp.where(me == k, jnp.where(owner >= me, above, below), later)

    def finish(u):
        g = (2 * u) // pairs_per_group
        gate_copy(2 * u).wait()
        gate_copy(2 * u + 1).wait()
        carry = jnp.concatenate([carry_of(2 * u), carry_of(2 * u + 1)], axis=1)
        big[...] = jnp.dot(readout2[g], split_rows(carry), preferred_element_type=F32)
        for q in range(subs):
            at = pl.ds(q * SUB, SUB)
            summed = acc[u, at, :] + dec[u, at, :] * big[at, :]
            gate = jnp.concatenate([gbuf[2 * u, at, :], gbuf[2 * u + 1, at, :]], axis=1)
            half = 0.5 * gate.astype(F32)
            gated = summed * (half + half * jnp.tanh(half))
            squares[at, :] = (gated * gated).astype(BF16)
            acc[u, at, :] = gated
        big[...] = jnp.dot(squares[...], mean_of, preferred_element_type=F32)
        norm_row = jnp.concatenate(
            [norm_ref[pl.ds(2 * u, 1), :], norm_ref[pl.ds(2 * u + 1, 1), :]], axis=1
        )
        for q in range(subs):
            at = pl.ds(q * SUB, SUB)
            normed = (acc[u, at, :] * lax.rsqrt(big[at, :] + 1e-5) * norm_row).astype(BF16)
            obuf[2 * u, at, :] = normed[:, :PAIR]
            obuf[2 * u + 1, at, :] = normed[:, PAIR:]
        out_copy(2 * u).start()
        out_copy(2 * u + 1).start()

    units = pairs // 2
    carry_lag = jnp.minimum(units, jnp.where(me == last, me + 1, me))
    finish_lag = jnp.where(relays, carry_lag + 2, carry_lag)

    @pl.loop(0, units + finish_lag)
    def _(step):
        @pl.when(step < units)
        def _():
            @pl.when(relays & (me >= 2))
            def _():
                back_step(2 * step)
                back_step(2 * step + 1)

            stage_one(step)

        @pl.when((step >= carry_lag) & (step < units + carry_lag))
        def _():
            carry_step(2 * (step - carry_lag))
            carry_step(2 * (step - carry_lag) + 1)

        @pl.when(step >= finish_lag)
        def _():
            finish(step - finish_lag)

    @pl.loop(0, pairs)
    def _(c):
        out_copy(c).wait()

        @pl.when(me >= 2)
        def _():
            back_copy(own, c).wait_send()

        @pl.when(me < last)
        def _():
            forward_copy(fsend, c).wait_send()


def on_device(
    n_seq,
    head_values,
    gate_values,
    state_inputs,
    state_readout,
    log_decays,
    skip_gains,
    norm_gains,
    cached_states,
    owner_slots,
    prefix_blocks,
    prompt_sessions,
):
    _, block, width = head_values.shape
    heads = width // HEAD_DIM
    per_group = HEAD_COUNT // GROUPS
    groups = max(1, heads // per_group)
    pairs = heads // 2
    subs = block // SUB
    owned = cached_states.shape[0]
    smem = pl.BlockSpec(memory_space=pltpu.SMEM)
    vmem = pl.BlockSpec(memory_space=pltpu.VMEM)
    hbm = pl.BlockSpec(memory_space=pl.ANY)
    sent = pltpu.VMEM((pairs, STATE + 8, PAIR), F32)
    tiles = pltpu.VMEM((pairs, STATE, PAIR), F32)
    sems = pltpu.SemaphoreType.DMA((pairs,))
    out, live = pl.pallas_call(
        functools.partial(kernel, n_seq, pairs, pairs // groups, per_group, subs, owned),
        out_shape=(
            jax.ShapeDtypeStruct(head_values.shape, BF16),
            jax.ShapeDtypeStruct((1,), jnp.int32),
        ),
        in_specs=[smem] * 4 + [vmem] * 5 + [hbm] * 2,
        out_specs=(hbm, smem),
        scratch_shapes=[
            pltpu.VMEM((pairs, block, PAIR), BF16),
            pltpu.VMEM((pairs, block, PAIR), BF16),
            pltpu.VMEM((pairs, block, PAIR), BF16),
            pltpu.VMEM((pairs // 2, block, QUAD), F32),
            pltpu.VMEM((pairs // 2, block, QUAD), F32),
            tiles, tiles, tiles, sent, sent, tiles,
            pltpu.VMEM((pairs, 8, PAIR), F32),
            pltpu.VMEM((block, 128), BF16),
            pltpu.VMEM((subs, heads, SUB), F32),
            pltpu.VMEM((128, SUB), F32),
            pltpu.VMEM((groups, subs, SUB, SUB), F32),
            pltpu.VMEM((groups, subs, STATE, SUB), BF16),
            pltpu.VMEM((groups, block, 2 * STATE), BF16),
            pltpu.VMEM((block, 4 * SUB), F32),
            pltpu.VMEM((block, QUAD), F32),
            pltpu.VMEM((block, QUAD), BF16),
            pltpu.VMEM((2, SUB * state_inputs.shape[2], STATE), F32),
            sems, sems, sems, sems, sems, sems, sems,
        ],
        compiler_params=pltpu.CompilerParams(
            collective_id=0, has_side_effects=True, vmem_limit_bytes=58 * 1024 * 1024
        ),
        name="scan_chain",
    )(
        prompt_sessions, owner_slots, prefix_blocks, skip_gains,
        state_inputs[0], state_readout[0], log_decays[0].T, norm_gains.reshape(pairs, PAIR),
        cached_states.reshape(owned, pairs, PAIR, STATE), head_values, gate_values,
    )
    return jnp.where(live[0] > 0, out, jnp.zeros_like(out))


def solution(mesh):
    in_specs = (
        P("groups", "seq", ("head", "cache")),
        P("groups", "seq", ("head", "cache")),
        P("groups", "seq", "head", None),
        P("groups", "seq", "head", None),
        P("groups", "seq", ("head", "cache")),
        P(("head", "cache")),
        P(("head", "cache")),
        P(("groups", "seq"), ("head", "cache"), None, None),
        P("groups"),
        P("groups"),
        P("groups"),
    )
    return jax.shard_map(
        functools.partial(on_device, mesh.shape["seq"]), mesh=mesh, in_specs=in_specs,
        out_specs=P("groups", "seq", ("head", "cache")), check_vma=False,
    )
```

```python
import functools

import jax
import jax.numpy as jnp
from jax import lax
from jax.experimental import pallas as pl
from jax.experimental.pallas import tpu as pltpu
from jax.sharding import PartitionSpec as P

HEAD_COUNT = 128
HEAD_DIM = 64
STATE = 128
GROUPS = 8
SUB = 128
PAIR = 2 * HEAD_DIM
LOG2E = 1.4426950408889634
QUAD = 2 * PAIR
F32 = jnp.float32
BF16 = jnp.bfloat16
MESH = pl.DeviceIdType.MESH


def split_rows(x):
    high = x.astype(BF16)
    low = (x - high.astype(F32)).astype(BF16)
    return jnp.concatenate([high, low], axis=0)


def kernel(
    n_seq, pairs, pairs_per_group, per_group, subs, owned_rows,
    sessions_ref, slots_ref, prefix_ref, skip_ref,
    *refs,
):
    me = lax.axis_index("seq")
    heads = 2 * pairs
    groups = pairs // pairs_per_group
    first_group = lax.axis_index("cache") * heads // per_group
    (
        inputs_ref, readout_ref, decays_ref, norm_ref, cached_ref, values_hbm, gates_hbm, out_hbm, live_ref,
        vbuf, gbuf, obuf, acc, dec, own, bsend, brecv, fsend, frecv, local, ending,
        cum3, cum_t, cum_pad, scores, inputs_t, readout2, spread, big, squares, staged,
        vsem, gsem, osem, bsend_sem, brecv_sem, fsend_sem, frecv_sem,
    ) = refs
    last = n_seq - 1

    def value_copy(c):
        return pltpu.make_async_copy(
            values_hbm.at[0, :, pl.ds(pl.multiple_of(c * PAIR, PAIR), PAIR)], vbuf.at[c], vsem.at[c]
        )

    def gate_copy(c):
        return pltpu.make_async_copy(
            gates_hbm.at[0, :, pl.ds(pl.multiple_of(c * PAIR, PAIR), PAIR)], gbuf.at[c], gsem.at[c]
        )

    def out_copy(c):
        return pltpu.make_async_copy(
            obuf.at[c], out_hbm.at[0, :, pl.ds(pl.multiple_of(c * PAIR, PAIR), PAIR)], osem.at[c]
        )

    def back_copy(src, c):
        return pltpu.make_async_remote_copy(
            src_ref=src.at[c], dst_ref=brecv.at[c], send_sem=bsend_sem.at[c],
            recv_sem=brecv_sem.at[c], device_id={"seq": me - 1}, device_id_type=MESH,
        )

    def forward_copy(src, c):
        return pltpu.make_async_remote_copy(
            src_ref=src.at[c], dst_ref=frecv.at[c], send_sem=fsend_sem.at[c],
            recv_sem=frecv_sem.at[c], device_id={"seq": me + 1}, device_id_type=MESH,
        )

    barrier = pltpu.get_barrier_semaphore()

    @pl.when(me > 0)
    def _():
        pl.semaphore_signal(barrier, inc=1, device_id={"seq": me - 1}, device_id_type=MESH)

    @pl.when(me < last)
    def _():
        pl.semaphore_signal(barrier, inc=1, device_id={"seq": me + 1}, device_id_type=MESH)

    @pl.loop(0, pairs)
    def _(c):
        value_copy(c).start()
        gate_copy(c).start()

    session = sessions_ref[0]
    slot = slots_ref[session]
    k = prefix_ref[session]
    owner = slot // owned_rows
    row_here = slot % owned_rows
    live_ref[0] = (me >= k).astype(jnp.int32)

    @pl.when((me > 0) & (me < last))
    def _():
        pl.semaphore_wait(barrier, 2)

    @pl.when((me == 0) | (me == last))
    def _():
        pl.semaphore_wait(barrier, 1)

    @pl.loop(0, pairs)
    def _(c):
        row = cached_ref[0, c]
        for other in range(1, owned_rows):
            row = jnp.where(row_here == other, cached_ref[other, c], row)
        row = row.T
        own[c] = row

        @pl.when(me == last)
        def _():
            bsend[c] = row
            back_copy(own, c).start()

        @pl.when(me == 0)
        def _():
            bsend[c] = row
            frecv[c] = jnp.zeros((STATE + 8, PAIR), F32)
            fsend[c, :STATE, :] = row
            fsend[c, STATE:, :] = jnp.zeros((8, PAIR), F32)
            forward_copy(fsend, c).start()

    rows = lax.broadcasted_iota(jnp.int32, (SUB, SUB), 0)
    lanes = lax.broadcasted_iota(jnp.int32, (SUB, SUB), 1)
    causal = rows >= lanes
    tri = jnp.where(rows <= lanes, 1.0, 0.0).astype(F32)
    cum_pad[...] = jnp.zeros_like(cum_pad)
    for q in range(subs):
        at = pl.ds(q * SUB, SUB)
        sums = jnp.dot(
            decays_ref[:, at] * LOG2E, tri, precision=lax.Precision.HIGHEST,
            preferred_element_type=F32,
        )
        cum_t[q] = sums
        cum_pad[:heads, :] = sums
        cum = cum_pad[...].T
        high = cum.astype(BF16).astype(F32)
        middle = (cum - high).astype(BF16).astype(F32)
        low = (cum - high - middle).astype(BF16).astype(F32)
        cum3[at, :] = (
            high + pltpu.roll(middle, heads, axis=1) + pltpu.roll(low, 2 * heads, axis=1)
        ).astype(BF16)
        for which, raw in enumerate((inputs_ref, readout_ref)):
            staged[which] = raw[at].astype(F32).reshape(SUB * raw.shape[1], STATE)
        step = inputs_ref.shape[1]
        for g in range(groups):
            mine = pl.ds(first_group + g, SUB, stride=step)
            b_rows32 = staged[0, mine, :]
            b_rows = b_rows32.astype(BF16)
            c_rows = staged[1, mine, :].astype(BF16)
            product = lax.dot_general(
                c_rows, b_rows, (((1,), (1,)), ((), ())), preferred_element_type=F32
            )
            scores[g, q] = jnp.where(causal, product, 0.0)
            inputs_t[g, q] = b_rows32.T.astype(BF16)
            readout2[g, at, :] = jnp.concatenate([c_rows, c_rows], axis=1)

    wide_rows = lax.broadcasted_iota(jnp.int32, (QUAD, QUAD), 0)
    wide_lanes = lax.broadcasted_iota(jnp.int32, (QUAD, QUAD), 1)
    first_half = lanes < HEAD_DIM
    wide_half = (wide_lanes[:SUB] % PAIR) < HEAD_DIM
    row_half = wide_half[:1]
    spread_rows = lax.broadcasted_iota(jnp.int32, (128, 4 * SUB), 0)
    spread_lanes = lax.broadcasted_iota(jnp.int32, (128, 4 * SUB), 1)
    mean_of = jnp.where(
        wide_rows // HEAD_DIM == wide_lanes // HEAD_DIM, 1.0 / HEAD_DIM, 0.0
    ).astype(BF16)

    def stage_one(u):
        g = (2 * u) // pairs_per_group
        value_copy(2 * u).wait()
        value_copy(2 * u + 1).wait()
        wanted = 4 * u + spread_lanes // SUB
        pick = jnp.where(
            (spread_rows < 3 * heads) & ((spread_rows % heads) == wanted), 1.0, 0.0
        ).astype(BF16)
        spread[...] = jnp.dot(cum3[...], pick, preferred_element_type=F32)
        low_pair = jnp.where(row_half, skip_ref[4 * u], skip_ref[4 * u + 1])
        high_pair = jnp.where(row_half, skip_ref[4 * u + 2], skip_ref[4 * u + 3])
        skip_row = jnp.where(wide_lanes[:1] < PAIR, low_pair, high_pair)
        state = None
        offset = jnp.zeros((1, QUAD), F32)
        for q in range(subs):
            at = pl.ds(q * SUB, SUB)
            score = scores[g, q]
            intra, values, cums = [], [], []
            for p in range(2):
                cum0 = spread[at, 2 * p * SUB : (2 * p + 1) * SUB]
                cum1 = spread[at, (2 * p + 1) * SUB : (2 * p + 2) * SUB]
                row0 = cum_t[q, pl.ds(4 * u + 2 * p, 1), :]
                row1 = cum_t[q, pl.ds(4 * u + 2 * p + 1, 1), :]
                mix0 = score * jnp.exp2(jnp.minimum(cum0 - row0, 0.0))
                mix1 = score * jnp.exp2(jnp.minimum(cum1 - row1, 0.0))
                mix = jnp.concatenate([mix0.astype(BF16), mix1.astype(BF16)], axis=1)
                value32 = vbuf[2 * u + p, at, :].astype(F32)
                both = jnp.concatenate(
                    [
                        jnp.where(first_half, value32, 0.0).astype(BF16),
                        jnp.where(first_half, 0.0, value32).astype(BF16),
                    ],
                    axis=0,
                )
                intra.append(jnp.dot(mix, both, preferred_element_type=F32))
                values.append(value32)
                cums.append(jnp.where(first_half, cum0, cum1))
            value = jnp.concatenate(values, axis=1)
            cum_p = jnp.concatenate(cums, axis=1)
            total = jnp.concatenate(intra, axis=1) + skip_row * value
            end = cum_p[SUB - 1 :, :]
            decay = jnp.exp2(cum_p)
            if state is not None:
                total += decay * jnp.dot(
                    readout2[g, at, :], split_rows(state), preferred_element_type=F32
                )
            acc[u, at, :] = total
            dec[u, at, :] = decay * jnp.exp2(offset)
            scaled = (value * jnp.exp2(end - cum_p)).astype(BF16)
            here = jnp.dot(inputs_t[g, q], scaled, preferred_element_type=F32)
            state = here if state is None else jnp.exp2(end) * state + here
            offset = offset + end
        local[2 * u] = state[:, :PAIR]
        local[2 * u + 1] = state[:, PAIR:]
        final = jnp.exp2(offset)
        ending[2 * u] = jnp.broadcast_to(final[:, :PAIR], (8, PAIR))
        ending[2 * u + 1] = jnp.broadcast_to(final[:, PAIR:], (8, PAIR))

    def back_step(c):
        back_copy(own, c).wait_recv()
        bsend[c] = jnp.where(owner == me, own[c], brecv[c])

        @pl.when(me >= 2)
        def _():
            back_copy(bsend, c).start()

    relays = (me > 0) & (me < last)

    def carry_step(c):
        @pl.when(me > 0)
        def _():
            forward_copy(fsend, c).wait_recv()

        below = frecv[c, :STATE, :]
        factor = frecv[c, STATE:, :]

        @pl.when(relays)
        def _():
            cached = jnp.where(owner == me, own[c], below)
            added = jnp.where(owner == me, below + factor[:1] * own[c], below)
            start = jnp.where(me == k, jnp.where(owner <= me, cached, 0.0), added)
            onward = ending[c, :1, :] * start + local[c]
            fsend[c, :STATE, :] = jnp.where(me < k, cached, onward)
            fsend[c, STATE:, :] = ending[c] * jnp.where(me == k, 1.0, factor)
            forward_copy(fsend, c).start()

    def carry_of(c):
        @pl.when(me == 1)
        def _():
            back_step(c)

        below = frecv[c, :STATE, :]
        above = bsend[c]
        later = jnp.where(owner >= me, below + frecv[c, STATE : STATE + 1, :] * above, below)
        return jnp.where(me == k, jnp.where(owner >= me, above, below), later)

    def finish(u):
        g = (2 * u) // pairs_per_group
        gate_copy(2 * u).wait()
        gate_copy(2 * u + 1).wait()
        carry = jnp.concatenate([carry_of(2 * u), carry_of(2 * u + 1)], axis=1)
        big[...] = jnp.dot(readout2[g], split_rows(carry), preferred_element_type=F32)
        for q in range(subs):
            at = pl.ds(q * SUB, SUB)
            summed = acc[u, at, :] + dec[u, at, :] * big[at, :]
            gate = jnp.concatenate([gbuf[2 * u, at, :], gbuf[2 * u + 1, at, :]], axis=1)
            half = 0.5 * gate.astype(F32)
            gated = summed * (half + half * jnp.tanh(half))
            squares[at, :] = (gated * gated).astype(BF16)
            acc[u, at, :] = gated
        big[...] = jnp.dot(squares[...], mean_of, preferred_element_type=F32)
        norm_row = jnp.concatenate(
            [norm_ref[pl.ds(2 * u, 1), :], norm_ref[pl.ds(2 * u + 1, 1), :]], axis=1
        )
        for q in range(subs):
            at = pl.ds(q * SUB, SUB)
            normed = (acc[u, at, :] * lax.rsqrt(big[at, :] + 1e-5) * norm_row).astype(BF16)
            obuf[2 * u, at, :] = normed[:, :PAIR]
            obuf[2 * u + 1, at, :] = normed[:, PAIR:]
        out_copy(2 * u).start()
        out_copy(2 * u + 1).start()

    units = pairs // 2
    carry_lag = jnp.minimum(units, jnp.where(me == last, me + 1, me))
    finish_lag = jnp.where(relays, carry_lag + 4, carry_lag)

    @pl.loop(0, units + finish_lag)
    def _(step):
        @pl.when(step < units)
        def _():
            @pl.when(relays & (me >= 2))
            def _():
                back_step(2 * step)
                back_step(2 * step + 1)

            stage_one(step)

        @pl.when((step >= carry_lag) & (step < units + carry_lag))
        def _():
            carry_step(2 * (step - carry_lag))
            carry_step(2 * (step - carry_lag) + 1)

        @pl.when(step >= finish_lag)
        def _():
            finish(step - finish_lag)

    @pl.loop(0, pairs)
    def _(c):
        out_copy(c).wait()

        @pl.when(me >= 2)
        def _():
            back_copy(own, c).wait_send()

        @pl.when(me < last)
        def _():
            forward_copy(fsend, c).wait_send()


def on_device(
    n_seq,
    head_values,
    gate_values,
    state_inputs,
    state_readout,
    log_decays,
    skip_gains,
    norm_gains,
    cached_states,
    owner_slots,
    prefix_blocks,
    prompt_sessions,
):
    _, block, width = head_values.shape
    heads = width // HEAD_DIM
    per_group = HEAD_COUNT // GROUPS
    groups = max(1, heads // per_group)
    pairs = heads // 2
    subs = block // SUB
    owned = cached_states.shape[0]
    smem = pl.BlockSpec(memory_space=pltpu.SMEM)
    vmem = pl.BlockSpec(memory_space=pltpu.VMEM)
    hbm = pl.BlockSpec(memory_space=pl.ANY)
    sent = pltpu.VMEM((pairs, STATE + 8, PAIR), F32)
    tiles = pltpu.VMEM((pairs, STATE, PAIR), F32)
    sems = pltpu.SemaphoreType.DMA((pairs,))
    out, live = pl.pallas_call(
        functools.partial(kernel, n_seq, pairs, pairs // groups, per_group, subs, owned),
        out_shape=(
            jax.ShapeDtypeStruct(head_values.shape, BF16),
            jax.ShapeDtypeStruct((1,), jnp.int32),
        ),
        in_specs=[smem] * 4 + [vmem] * 5 + [hbm] * 2,
        out_specs=(hbm, smem),
        scratch_shapes=[
            pltpu.VMEM((pairs, block, PAIR), BF16),
            pltpu.VMEM((pairs, block, PAIR), BF16),
            pltpu.VMEM((pairs, block, PAIR), BF16),
            pltpu.VMEM((pairs // 2, block, QUAD), F32),
            pltpu.VMEM((pairs // 2, block, QUAD), F32),
            tiles, tiles, tiles, sent, sent, tiles,
            pltpu.VMEM((pairs, 8, PAIR), F32),
            pltpu.VMEM((block, 128), BF16),
            pltpu.VMEM((subs, heads, SUB), F32),
            pltpu.VMEM((128, SUB), F32),
            pltpu.VMEM((groups, subs, SUB, SUB), F32),
            pltpu.VMEM((groups, subs, STATE, SUB), BF16),
            pltpu.VMEM((groups, block, 2 * STATE), BF16),
            pltpu.VMEM((block, 4 * SUB), F32),
            pltpu.VMEM((block, QUAD), F32),
            pltpu.VMEM((block, QUAD), BF16),
            pltpu.VMEM((2, SUB * state_inputs.shape[2], STATE), F32),
            sems, sems, sems, sems, sems, sems, sems,
        ],
        compiler_params=pltpu.CompilerParams(
            collective_id=0, has_side_effects=True, vmem_limit_bytes=58 * 1024 * 1024
        ),
        name="scan_chain",
    )(
        prompt_sessions, owner_slots, prefix_blocks, skip_gains,
        state_inputs[0], state_readout[0], log_decays[0].T, norm_gains.reshape(pairs, PAIR),
        cached_states.reshape(owned, pairs, PAIR, STATE), head_values, gate_values,
    )
    return jnp.where(live[0] > 0, out, jnp.zeros_like(out))


def solution(mesh):
    in_specs = (
        P("groups", "seq", ("head", "cache")),
        P("groups", "seq", ("head", "cache")),
        P("groups", "seq", "head", None),
        P("groups", "seq", "head", None),
        P("groups", "seq", ("head", "cache")),
        P(("head", "cache")),
        P(("head", "cache")),
        P(("groups", "seq"), ("head", "cache"), None, None),
        P("groups"),
        P("groups"),
        P("groups"),
    )
    return jax.shard_map(
        functools.partial(on_device, mesh.shape["seq"]), mesh=mesh, in_specs=in_specs,
        out_specs=P("groups", "seq", ("head", "cache")), check_vma=False,
    )
```
